32 devices in a mesh: scan: 2 (over x), tile: 16 (over z, y, core).
Axes of the slice: x: 2, y: 2, z: 4, core: 2. Of those that a mesh axis runs over, the one named last changes fastest.
Arguments:
- slices: float32 [4, 2, 1024, 1024], P(None, None, ('scan', 'tile')), parts along dimension 2, may hold values from -4 to 4
- probe_modes: float32 [4, 2, 128, 128], P('scan'), parts along dimension 0, may hold values from -4 to 4
- row_offset: int32 [128], P(('scan', 'tile')), parts along dimension 0, may hold values from 0 to 31, as said below
- col_offset: int32 [128], P(('scan', 'tile')), parts along dimension 0, may hold values from 0 to 1023
- amplitude: float32 [128, 128, 128], P(('scan', 'tile')), parts along dimension 0, may hold values from 0.5 to 3
Outputs:
- slice_grad: float32 [4, 2, 1024, 1024], P(None, None, ('scan', 'tile')), parts along dimension 2
- probe_grad: float32 [4, 2, 128, 128], P('scan'), parts along dimension 0
The draws below stay inside these ranges and needn't reach their ends.
There are 2 independent parts, one for each index of `scan`. The reference program is written for one: setup_inputs(seed, part) draws one part's arguments, and reference() takes and returns one part's arrays. A program takes and returns all parts, laid end to end along the dimension named above; each array names one. Nothing has to cross between parts.
Inputs may be any that keep to these rules, and one draw needn't show every extreme that they name: Window w starts 32 * (w // 4) + row_offset[w] rows down the object; the largest value is taken by some window in every draw.
All inputs are finite; a program needn't handle non-finite values.
Results may differ from the reference program's by a relative error of at most 0.0003.
Values sent between devices are 32-bit elements; how exact they have to be, the bound alone decides.
A program may use at most 128 MiB of HBM per device.

```python
import math
import jax
import jax.numpy as jnp
from jax import lax

W = 128
MODES = 2
SLICES = 4
COLS = 1024
WIN_DEV = 4
ROWS_DEV = 32
NROWS = 512
WINDOWS = 64


def draw_row_offset(key, part):
    values = jax.random.randint(jax.random.fold_in(key, 11), (WINDOWS,), 0, ROWS_DEV, dtype=jnp.int32)
    spot_index = jax.random.randint(jax.random.fold_in(key, 12), (), 0, WINDOWS, dtype=jnp.int32)
    positions = jnp.arange(WINDOWS, dtype=jnp.int32)
    return jnp.where(positions == spot_index, ROWS_DEV - 1, values).astype(jnp.int32)


def set_ends(array, own_key, smallest, top_value):
    extent = array.shape
    place = [jax.random.randint(jax.random.fold_in(own_key, axis), (), 0, extent[axis]) for axis in range(len(extent))]
    array = array.at[tuple(place)].set(smallest)
    longest = extent.index(max(extent))
    place[longest] = (place[longest] + 1) % extent[longest]
    return array.at[tuple(place)].set(top_value)


def block_levels(stream_key, extent, cuts, low, top_value):
    loudness, own = 1.0, jax.random.fold_in(stream_key, 6)
    for dim, shards_of in cuts:
        heights = jnp.exp(jax.random.uniform(jax.random.fold_in(own, dim), (shards_of,), jnp.float32, low / len(cuts), top_value / len(cuts)))
        loudness = loudness * jnp.repeat(heights, extent[dim] // shards_of).reshape([-1 if axis == dim else 1 for axis in range(len(extent))])
    return loudness


def centred(rng, shape, scale, bound, cuts=(), kind=jnp.bfloat16):
    result = jax.random.normal(rng, shape, jnp.float32) * scale
    if len(cuts) > 0:
        result = block_levels(rng, shape, cuts, -0.22, 0.18) * result
    return jnp.clip(result, min=-bound, max=bound).astype(kind)


def setup_inputs(seed: int = 0, part: int = 0) -> dict:
    arg_keys = jax.random.split(jax.random.key(seed), 6)
    own_keys = jax.random.split(jax.random.fold_in(arg_keys[5], part), 6)
    slices = centred(own_keys[0], (SLICES, 2, NROWS, COLS), 0.7, 4.0, ((2, 16),), jnp.float32)
    probe_modes = centred(own_keys[1], (MODES, 2, W, W), 0.7, 4.0, (), jnp.float32)
    row_offset = draw_row_offset(jax.random.fold_in(jax.random.fold_in(arg_keys[5], part), 71), part)
    col_offset = set_ends(jax.random.randint(own_keys[3], (WINDOWS,), 0, COLS), jax.random.fold_in(own_keys[3], 1), 0, COLS - 1).astype(jnp.int32)
    amplitude = jnp.clip(jnp.exp(math.log(3.0) - 1.7917595 * jax.random.uniform(own_keys[4], (WINDOWS, W, W), jnp.float32) ** block_levels(own_keys[4], (WINDOWS, W, W), ((0, 16),), -0.2, 0.2)), 0.5, 3.0)
    return {"slices": slices, "probe_modes": probe_modes, "row_offset": row_offset, "col_offset": col_offset, "amplitude": amplitude}


INTENSITY_SHIFT = 0.5
FRESNEL = 0.75

def dft_tables(window_side):
    steps_idx = jnp.arange(window_side, dtype=jnp.int32)
    product = steps_idx[:, None] * steps_idx[None, :] % window_side
    angles = product.astype(jnp.float32) * (-2.0 * math.pi / window_side)
    scale = 1.0 / math.sqrt(window_side)
    return (jnp.cos(angles) * scale, jnp.sin(angles) * scale)

def fresnel_kernel(window_side):
    steps_idx = jnp.arange(window_side, dtype=jnp.int32)
    freqs = (steps_idx + window_side // 2) % window_side - window_side // 2
    radius = (freqs[:, None] * freqs[:, None] + freqs[None, :] * freqs[None, :]).astype(jnp.float32)
    phase = radius * (-math.pi * FRESNEL / (window_side / 2.0) ** 2)
    return (jnp.cos(phase), jnp.sin(phase))

def left_apply(mat_real, mat_imag, wave_real, wave_imag):

    def product(matrix, field):
        return jnp.einsum('jk,mkl->mjl', matrix, field, precision=lax.Precision.HIGHEST)
    return (product(mat_real, wave_real) - product(mat_imag, wave_imag), product(mat_real, wave_imag) + product(mat_imag, wave_real))

def right_apply(wave_real, wave_imag, mat_real, mat_imag):

    def product(field, matrix):
        return jnp.einsum('mjk,kl->mjl', field, matrix, precision=lax.Precision.HIGHEST)
    return (product(wave_real, mat_real) - product(wave_imag, mat_imag), product(wave_imag, mat_real) + product(wave_real, mat_imag))

def transform(wave_real, wave_imag, mat_real, mat_imag):
    half_real, half_imag = left_apply(mat_real, mat_imag, wave_real, wave_imag)
    return right_apply(half_real, half_imag, mat_real, mat_imag)

def propagate(wave_real, wave_imag, tables):
    cos_table, sin_table, kernel_real, kernel_imag = tables
    spec_real, spec_imag = transform(wave_real, wave_imag, cos_table, sin_table)
    moved_real = spec_real * kernel_real - spec_imag * kernel_imag
    moved_imag = spec_real * kernel_imag + spec_imag * kernel_real
    return transform(moved_real, moved_imag, cos_table, -sin_table)

def window_loss(crops, probe_modes, measured, tables):
    cos_table, sin_table = (tables[0], tables[1])
    wave_real = probe_modes[:, 0]
    wave_imag = probe_modes[:, 1]
    slice_count = crops.shape[0]
    exit_real = wave_real
    exit_imag = wave_imag
    for depth_index in range(slice_count):
        trans_real = crops[depth_index, 0]
        trans_imag = crops[depth_index, 1]
        exit_real = trans_real * wave_real - trans_imag * wave_imag
        exit_imag = trans_real * wave_imag + trans_imag * wave_real
        if depth_index + 1 < slice_count:
            wave_real, wave_imag = propagate(exit_real, exit_imag, tables)
    far_real, far_imag = transform(exit_real, exit_imag, cos_table, sin_table)
    intensity = lax.optimization_barrier(jnp.sum(far_real * far_real + far_imag * far_imag, axis=0))
    modelled = jnp.sqrt(intensity + INTENSITY_SHIFT)
    return 0.5 * jnp.sum((modelled - measured) ** 2)

def window_grads(crops, probe_modes, measured, tables):
    return jax.grad(window_loss, argnums=(0, 1))(crops, probe_modes, measured, tables)

def reference(slices, probe_modes, row_offset, col_offset, amplitude):
    window_side = probe_modes.shape[-1]
    total_rows = slices.shape[2]
    total_cols = slices.shape[3]
    cos_table, sin_table = dft_tables(window_side)
    kernel_real, kernel_imag = fresnel_kernel(window_side)
    tables = (cos_table, sin_table, kernel_real, kernel_imag)
    wrapped = jnp.concatenate([slices, slices[:, :, :window_side - 1]], axis=2)
    wrapped = jnp.concatenate([wrapped, wrapped[:, :, :, :window_side - 1]], axis=3)
    owners = jnp.arange(WINDOWS, dtype=jnp.int32) // WIN_DEV
    row_starts = (owners * ROWS_DEV + row_offset).astype(jnp.int32)
    anchor = jnp.zeros((), jnp.int32)

    def visit(state, inputs):
        slice_acc, probe_acc = state
        row_start, col_start, measured = inputs
        corner = (anchor, anchor, row_start.astype(jnp.int32), col_start.astype(jnp.int32))
        crops = lax.dynamic_slice(wrapped, corner, (SLICES, 2, window_side, window_side))
        crop_grad, probe_term = window_grads(crops, probe_modes, measured, tables)
        current = lax.dynamic_slice(slice_acc, corner, (SLICES, 2, window_side, window_side))
        slice_acc = lax.dynamic_update_slice(slice_acc, current + crop_grad, corner)
        return ((slice_acc, probe_acc + probe_term), None)
    initial = (jnp.zeros(wrapped.shape, jnp.float32), jnp.zeros(probe_modes.shape, jnp.float32))
    (slice_acc, probe_grad), _ = lax.scan(visit, initial, (row_starts, col_offset, amplitude))
    folded = slice_acc[:, :, :total_rows].at[:, :, :window_side - 1].add(slice_acc[:, :, total_rows:])
    folded = folded[:, :, :, :total_cols].at[:, :, :, :window_side - 1].add(folded[:, :, :, total_cols:])
    return (folded, probe_grad)
```

```python
import functools
import math

import jax
import jax.numpy as jnp
import numpy as np
from jax import lax
from jax.experimental import pallas as pl
from jax.experimental.pallas import tpu as pltpu
from jax.sharding import PartitionSpec as P

INTENSITY_SHIFT = 0.5
FRESNEL = 0.75
LANES = 128
SUBLANES = 8


def field_tables(side):
    idx = np.arange(side)
    fourier = np.exp(-2j * np.pi * (np.outer(idx, idx) % side) / side) / np.sqrt(side)
    freq = (idx + side // 2) % side - side // 2
    line = np.exp(-1j * np.pi * FRESNEL * freq**2 / (side / 2.0) ** 2)
    propagator = fourier.conj() @ (line[:, None] * fourier)
    blocks = []
    for matrix in (propagator, fourier, fourier.conj(), propagator.conj()):
        block = np.block([[matrix.real, matrix.imag], [-matrix.imag, matrix.real]])
        high = block.astype(np.float32).astype(jnp.bfloat16)
        low = (block - high.astype(np.float64)).astype(np.float32).astype(jnp.bfloat16)
        blocks.append(np.stack([high, low]))
    return np.stack(blocks)


PROP, FWD, INV, PROP_ADJ = range(4)
CONJ = {PROP: PROP_ADJ, FWD: INV, INV: FWD, PROP_ADJ: PROP}


def split_pair(value):
    high = value.astype(jnp.bfloat16)
    low = (value - high.astype(jnp.float32)).astype(jnp.bfloat16)
    return high, low


def two_sided(table_ref, which, fields, side):
    right_high, right_low = table_ref[which, 0], table_ref[which, 1]
    right_mat = jnp.concatenate([right_high, right_low, right_high], axis=0)
    halves = []
    for modes in fields:
        rows = jnp.concatenate([jnp.concatenate([re, im], axis=1) for re, im in modes], axis=0)
        high, low = split_pair(rows)
        lhs = jnp.concatenate([high, high, low], axis=1)
        halves.append(jnp.dot(lhs, right_mat, preferred_element_type=jnp.float32))
    left_high, left_low = table_ref[CONJ[which], 0], table_ref[CONJ[which], 1]
    left_mat = jnp.concatenate([left_high, left_high, left_low], axis=1)
    results = []
    for half, modes in zip(halves, fields):
        count = len(modes)
        high, low = split_pair(half)

        def stack(part):
            pieces = [part[m * side : (m + 1) * side] for m in range(count)]
            return jnp.concatenate(
                [
                    jnp.concatenate([p[:, :side] for p in pieces], axis=1),
                    jnp.concatenate([p[:, side:] for p in pieces], axis=1),
                ],
                axis=0,
            )

        high, low = stack(high), stack(low)
        rhs = jnp.concatenate([high, low, high], axis=0)
        full = jnp.dot(left_mat, rhs, preferred_element_type=jnp.float32)
        results.append(
            [
                (full[:side, m * side : (m + 1) * side], full[side:, m * side : (m + 1) * side])
                for m in range(count)
            ]
        )
    return results


def window_kernel(pieces_count, row_ref, col_ref, *refs):
    pieces = refs[:pieces_count]
    probe_ref, amp_ref, table_ref = refs[pieces_count : pieces_count + 3]
    outs = refs[pieces_count + 3 : 2 * pieces_count + 3]
    probe_out = refs[2 * pieces_count + 3]
    ext, grad, crops, waves, in_sem, out_sem = refs[2 * pieces_count + 4 :]
    slice_count, _, rows_here, cols_here = pieces[0].shape
    windows, side = amp_ref.shape[0], amp_ref.shape[1]
    modes = probe_ref.shape[0]
    col_blocks = cols_here // LANES

    def incoming(s, o):
        return pltpu.make_async_copy(
            pieces[o].at[s], ext.at[s, :, pl.ds(o * rows_here, rows_here)], in_sem.at[s, o]
        )

    def outgoing(s, o):
        return pltpu.make_async_copy(
            grad.at[s, :, pl.ds(o * rows_here, rows_here)], outs[o].at[s], out_sem.at[s, o]
        )

    for s in range(slice_count):
        for o in range(pieces_count):
            incoming(s, o).start()
    grad[...] = jnp.zeros_like(grad)

    tall = side + SUBLANES
    lane = lax.broadcasted_iota(jnp.int32, (tall, LANES), 1)
    margin = jnp.zeros((SUBLANES, LANES), jnp.float32)
    places = []
    for w in range(windows):
        row, col = row_ref[w], col_ref[w]
        block = col // LANES
        shift = col - block * LANES
        first = pl.multiple_of(block * LANES, LANES)
        second = pl.multiple_of(lax.rem(block + 1, col_blocks) * LANES, LANES)
        base = row // SUBLANES * SUBLANES
        places.append((pl.multiple_of(base, SUBLANES), row - base, first, second, shift))

    fields = [[(probe_ref[m, 0], probe_ref[m, 1]) for m in range(modes)] for _ in range(windows)]
    for s in range(slice_count):
        for o in range(pieces_count):
            incoming(s, o).wait()
        exits = []
        for w in range(windows):
            row, lift, first, second, shift = places[w]
            back = lax.rem(LANES - shift, LANES)
            planes = []
            for c in range(2):
                one = pltpu.roll(ext[s, c, pl.ds(row, tall), pl.ds(first, LANES)], back, 1)
                two = pltpu.roll(ext[s, c, pl.ds(row, tall), pl.ds(second, LANES)], back, 1)
                plane = jnp.where(lane < LANES - shift, one, two)
                plane = pltpu.roll(plane, lax.rem(tall - lift, tall), 0)[:side]
                crops[s, w, c] = plane
                planes.append(plane)
            obj_re, obj_im = planes
            chi = []
            for m in range(modes):
                re, im = fields[w][m]
                chi.append((obj_re * re - obj_im * im, obj_re * im + obj_im * re))
            exits.append(chi)
        fields = two_sided(table_ref, PROP if s + 1 < slice_count else FWD, exits, side)
        if s + 1 < slice_count:
            for w in range(windows):
                for m in range(modes):
                    waves[s, w, m, 0] = fields[w][m][0]
                    waves[s, w, m, 1] = fields[w][m][1]

    far_grads = []
    for w in range(windows):
        intensity = sum(re * re + im * im for re, im in fields[w])
        factor = 1.0 - amp_ref[w] / jnp.sqrt(intensity + INTENSITY_SHIFT)
        far_grads.append([(factor * re, factor * im) for re, im in fields[w]])
    fields = two_sided(table_ref, INV, far_grads, side)

    for s in reversed(range(slice_count)):
        wave_grads = []
        for w in range(windows):
            row, lift, first, second, shift = places[w]
            obj_re, obj_im = crops[s, w, 0], crops[s, w, 1]
            grad_re = jnp.zeros((side, side), jnp.float32)
            grad_im = jnp.zeros((side, side), jnp.float32)
            terms = []
            for m in range(modes):
                re, im = fields[w][m]
                if s == 0:
                    wave_re, wave_im = probe_ref[m, 0], probe_ref[m, 1]
                else:
                    wave_re, wave_im = waves[s - 1, w, m, 0], waves[s - 1, w, m, 1]
                grad_re += re * wave_re + im * wave_im
                grad_im += im * wave_re - re * wave_im
                terms.append((re * obj_re + im * obj_im, im * obj_re - re * obj_im))
            wave_grads.append(terms)
            for c, plane in enumerate((grad_re, grad_im)):
                turned = pltpu.roll(jnp.concatenate([plane, margin], axis=0), lift, 0)
                turned = pltpu.roll(turned, shift, 1)
                low = jnp.where(lane >= shift, turned, 0.0)
                grad[s, c, pl.ds(row, tall), pl.ds(first, LANES)] += low
                high = jnp.where(lane < shift, turned, 0.0)
                grad[s, c, pl.ds(row, tall), pl.ds(second, LANES)] += high
        for o in range(pieces_count):
            outgoing(s, o).start()
        if s > 0:
            fields = two_sided(table_ref, PROP_ADJ, wave_grads, side)
    for m in range(modes):
        for c in range(2):
            probe_out[m, c] = sum(wave_grads[w][m][c] for w in range(windows))
    for s in range(slice_count):
        for o in range(pieces_count):
            outgoing(s, o).wait()


def run_windows(pieces, probe_modes, row_offset, col_offset, amplitude):
    count = len(pieces)
    slice_count, parts, rows_here, cols_here = pieces[0].shape
    windows, side = amplitude.shape[0], amplitude.shape[1]
    modes = probe_modes.shape[0]
    tables = jnp.asarray(field_tables(side))
    anywhere = pl.BlockSpec(memory_space=pl.ANY)
    vmem = pl.BlockSpec(memory_space=pltpu.VMEM)
    smem = pl.BlockSpec(memory_space=pltpu.SMEM)
    total = count * rows_here
    return pl.pallas_call(
        functools.partial(window_kernel, count),
        out_shape=[jax.ShapeDtypeStruct(p.shape, jnp.float32) for p in pieces]
        + [jax.ShapeDtypeStruct(probe_modes.shape, jnp.float32)],
        in_specs=[smem, smem] + [anywhere] * count + [vmem] * 3,
        out_specs=[anywhere] * count + [vmem],
        scratch_shapes=[
            pltpu.VMEM((slice_count, parts, total, cols_here), jnp.float32),
            pltpu.VMEM((slice_count, parts, total, cols_here), jnp.float32),
            pltpu.VMEM((slice_count, windows, parts, side, side), jnp.float32),
            pltpu.VMEM((slice_count - 1, windows, modes, 2, side, side), jnp.float32),
            pltpu.SemaphoreType.DMA((slice_count, count)),
            pltpu.SemaphoreType.DMA((slice_count, count)),
        ],
        compiler_params=pltpu.CompilerParams(vmem_limit_bytes=48 << 20),
        name="windows",
    )(row_offset, col_offset, *pieces, probe_modes, amplitude, tables)


def permute(value, pairs):
    return lax.ppermute(value, "tile", pairs)


def on_device(slices, probe_modes, row_offset, col_offset, amplitude):
    side = probe_modes.shape[-1]
    rows_here = slices.shape[2]
    reach = (side - 2) // rows_here + 1
    assert reach == 4
    tiles = lax.axis_size("tile")
    index = lax.axis_index("tile")
    core = index % 2
    odd_chip = (index // 2) % 2
    swap_core = [(s, s ^ 1) for s in range(tiles)]
    swap_chip = [(s, s ^ 2) for s in range(tiles)]
    ahead = [(s, (s - 4) % tiles) for s in range(tiles)]
    behind = [(s, (s + 4) % tiles) for s in range(tiles)]

    fourth = permute(slices, ahead)
    second = permute(jnp.where(odd_chip == 1, slices, fourth), swap_chip)
    first = permute(jnp.where(core == 1, slices, second), swap_core)
    third = permute(jnp.where(core == 1, second, fourth), swap_core)
    pieces = [slices, first, second, third, fourth]

    *shares, probe_terms = run_windows(pieces, probe_modes, row_offset, col_offset, amplitude)

    got_first = permute(shares[1], swap_core)
    got_third = permute(shares[3], swap_core)
    low_core = core == 0
    sum_second = shares[2] + jnp.where(low_core, got_first, got_third)
    got_second = permute(sum_second, swap_chip)
    even = odd_chip == 0
    sum_fourth = shares[4] + jnp.where(low_core, got_third, 0.0) + jnp.where(even, got_second, 0.0)
    own = shares[0] + jnp.where(low_core, 0.0, got_first) + jnp.where(even, 0.0, got_second)
    slice_grad = own + permute(sum_fourth, behind)

    step = 1
    while step < tiles:
        probe_terms = probe_terms + permute(probe_terms, [(s, s ^ step) for s in range(tiles)])
        step *= 2
    return (slice_grad, probe_terms)


def solution(mesh):
    placed = (
        P(None, None, ("scan", "tile"), None),
        P("scan", None, None, None),
        P(("scan", "tile")),
        P(("scan", "tile")),
        P(("scan", "tile"), None, None),
    )
    return jax.shard_map(
        on_device,
        mesh=mesh,
        in_specs=placed,
        out_specs=(P(None, None, ("scan", "tile"), None), P("scan", None, None, None)),
        check_vma=False,
    )
```

```python
import functools

import jax
import jax.numpy as jnp
import numpy as np
from jax import lax
from jax.experimental import pallas as pl
from jax.experimental.pallas import tpu as pltpu
from jax.sharding import PartitionSpec as P

INTENSITY_SHIFT = 0.5
FRESNEL = 0.75
LANES = 128
SUBLANES = 8


def field_tables(side):
    idx = np.arange(side)
    fourier = np.exp(-2j * np.pi * (np.outer(idx, idx) % side) / side) / np.sqrt(side)
    freq = (idx + side // 2) % side - side // 2
    line = np.exp(-1j * np.pi * FRESNEL * freq**2 / (side / 2.0) ** 2)
    propagator = fourier.conj() @ (line[:, None] * fourier)
    blocks = []
    for matrix in (propagator, fourier, fourier.conj(), propagator.conj()):
        block = np.block([[matrix.real, matrix.imag], [-matrix.imag, matrix.real]])
        high = block.astype(np.float32).astype(jnp.bfloat16)
        low = (block - high.astype(np.float64)).astype(np.float32).astype(jnp.bfloat16)
        blocks.append(np.stack([high, low]))
    return np.stack(blocks)


PROP, FWD, INV, PROP_ADJ = range(4)
CONJ = {PROP: PROP_ADJ, FWD: INV, INV: FWD, PROP_ADJ: PROP}


def split_pair(value):
    high = value.astype(jnp.bfloat16)
    low = (value - high.astype(jnp.float32)).astype(jnp.bfloat16)
    return high, low


def two_sided(table_ref, which, fields, side):
    right_high, right_low = table_ref[which, 0], table_ref[which, 1]
    right_mat = jnp.concatenate([right_high, right_low, right_high], axis=0)
    halves = []
    for modes in fields:
        rows = jnp.concatenate([jnp.concatenate([re, im], axis=1) for re, im in modes], axis=0)
        high, low = split_pair(rows)
        lhs = jnp.concatenate([high, high, low], axis=1)
        halves.append(jnp.dot(lhs, right_mat, preferred_element_type=jnp.float32))
    left_high, left_low = table_ref[CONJ[which], 0], table_ref[CONJ[which], 1]
    left_mat = jnp.concatenate([left_high, left_high, left_low], axis=1)
    results = []
    for half, modes in zip(halves, fields):
        count = len(modes)
        high, low = split_pair(half)

        def stack(part):
            pieces = [part[m * side : (m + 1) * side] for m in range(count)]
            return jnp.concatenate(
                [
                    jnp.concatenate([p[:, :side] for p in pieces], axis=1),
                    jnp.concatenate([p[:, side:] for p in pieces], axis=1),
                ],
                axis=0,
            )

        high, low = stack(high), stack(low)
        rhs = jnp.concatenate([high, low, high], axis=0)
        full = jnp.dot(left_mat, rhs, preferred_element_type=jnp.float32)
        results.append(
            [
                (full[:side, m * side : (m + 1) * side], full[side:, m * side : (m + 1) * side])
                for m in range(count)
            ]
        )
    return results


def window_kernel(pieces_count, row_ref, col_ref, *refs):
    pieces = refs[:pieces_count]
    probe_ref, amp_ref, table_ref = refs[pieces_count : pieces_count + 3]
    outs = refs[pieces_count + 3 : 2 * pieces_count + 3]
    probe_out = refs[2 * pieces_count + 3]
    ext, grad, crops, waves, in_sem, out_sem = refs[2 * pieces_count + 4 :]
    slice_count, _, rows_here, cols_here = pieces[0].shape
    windows, side = amp_ref.shape[0], amp_ref.shape[1]
    modes = probe_ref.shape[0]
    col_blocks = cols_here // LANES

    def incoming(s, o):
        return pltpu.make_async_copy(
            pieces[o].at[s], ext.at[s, :, pl.ds(o * rows_here, rows_here)], in_sem.at[s, o]
        )

    def outgoing(s, o):
        return pltpu.make_async_copy(
            grad.at[s, :, pl.ds(o * rows_here, rows_here)], outs[o].at[s], out_sem.at[s, o]
        )

    for s in range(slice_count):
        for o in range(pieces_count):
            incoming(s, o).start()
    grad[...] = jnp.zeros_like(grad)

    tall = side + SUBLANES
    lane = lax.broadcasted_iota(jnp.int32, (tall, LANES), 1)
    margin = jnp.zeros((SUBLANES, LANES), jnp.float32)
    places = []
    for w in range(windows):
        row, col = row_ref[w], col_ref[w]
        block = col // LANES
        shift = col - block * LANES
        first = pl.multiple_of(block * LANES, LANES)
        second = pl.multiple_of(lax.rem(block + 1, col_blocks) * LANES, LANES)
        base = row // SUBLANES * SUBLANES
        places.append((pl.multiple_of(base, SUBLANES), row - base, first, second, shift))

    fields = [[(probe_ref[m, 0], probe_ref[m, 1]) for m in range(modes)] for _ in range(windows)]
    for s in range(slice_count):
        for o in range(pieces_count):
            incoming(s, o).wait()
        exits = []
        for w in range(windows):
            row, lift, first, second, shift = places[w]
            back = lax.rem(LANES - shift, LANES)
            planes = []
            for c in range(2):
                one = pltpu.roll(ext[s, c, pl.ds(row, tall), pl.ds(first, LANES)], back, 1)
                two = pltpu.roll(ext[s, c, pl.ds(row, tall), pl.ds(second, LANES)], back, 1)
                plane = jnp.where(lane < LANES - shift, one, two)
                plane = pltpu.roll(plane, lax.rem(tall - lift, tall), 0)[:side]
                crops[s, w, c] = plane
                planes.append(plane)
            obj_re, obj_im = planes
            chi = []
            for m in range(modes):
                re, im = fields[w][m]
                chi.append((obj_re * re - obj_im * im, obj_re * im + obj_im * re))
            exits.append(chi)
        fields = two_sided(table_ref, PROP if s + 1 < slice_count else FWD, exits, side)
        if s + 1 < slice_count:
            for w in range(windows):
                for m in range(modes):
                    waves[s, w, m, 0] = fields[w][m][0]
                    waves[s, w, m, 1] = fields[w][m][1]

    far_grads = []
    for w in range(windows):
        intensity = sum(re * re + im * im for re, im in fields[w])
        factor = 1.0 - amp_ref[w] / jnp.sqrt(intensity + INTENSITY_SHIFT)
        far_grads.append([(factor * re, factor * im) for re, im in fields[w]])
    fields = two_sided(table_ref, INV, far_grads, side)

    for s in reversed(range(slice_count)):
        wave_grads = []
        for w in range(windows):
            row, lift, first, second, shift = places[w]
            obj_re, obj_im = crops[s, w, 0], crops[s, w, 1]
            grad_re = jnp.zeros((side, side), jnp.float32)
            grad_im = jnp.zeros((side, side), jnp.float32)
            terms = []
            for m in range(modes):
                re, im = fields[w][m]
                if s == 0:
                    wave_re, wave_im = probe_ref[m, 0], probe_ref[m, 1]
                else:
                    wave_re, wave_im = waves[s - 1, w, m, 0], waves[s - 1, w, m, 1]
                grad_re += re * wave_re + im * wave_im
                grad_im += im * wave_re - re * wave_im
                terms.append((re * obj_re + im * obj_im, im * obj_re - re * obj_im))
            wave_grads.append(terms)
            for c, plane in enumerate((grad_re, grad_im)):
                turned = pltpu.roll(jnp.concatenate([plane, margin], axis=0), lift, 0)
                turned = pltpu.roll(turned, shift, 1)
                low = jnp.where(lane >= shift, turned, 0.0)
                grad[s, c, pl.ds(row, tall), pl.ds(first, LANES)] += low
                high = jnp.where(lane < shift, turned, 0.0)
                grad[s, c, pl.ds(row, tall), pl.ds(second, LANES)] += high
        for o in range(pieces_count):
            outgoing(s, o).start()
        if s > 0:
            fields = two_sided(table_ref, PROP_ADJ, wave_grads, side)
    for m in range(modes):
        for c in range(2):
            probe_out[m, c] = sum(wave_grads[w][m][c] for w in range(windows))
    for s in range(slice_count):
        for o in range(pieces_count):
            outgoing(s, o).wait()


def run_windows(pieces, probe_modes, row_offset, col_offset, amplitude):
    count = len(pieces)
    slice_count, parts, rows_here, cols_here = pieces[0].shape
    windows, side = amplitude.shape[0], amplitude.shape[1]
    modes = probe_modes.shape[0]
    tables = jnp.asarray(field_tables(side))
    anywhere = pl.BlockSpec(memory_space=pl.ANY)
    vmem = pl.BlockSpec(memory_space=pltpu.VMEM)
    smem = pl.BlockSpec(memory_space=pltpu.SMEM)
    total = count * rows_here
    return pl.pallas_call(
        functools.partial(window_kernel, count),
        out_shape=[jax.ShapeDtypeStruct(p.shape, jnp.float32) for p in pieces]
        + [jax.ShapeDtypeStruct(probe_modes.shape, jnp.float32)],
        in_specs=[smem, smem] + [anywhere] * count + [vmem] * 3,
        out_specs=[anywhere] * count + [vmem],
        scratch_shapes=[
            pltpu.VMEM((slice_count, parts, total, cols_here), jnp.float32),
            pltpu.VMEM((slice_count, parts, total, cols_here), jnp.float32),
            pltpu.VMEM((slice_count, windows, parts, side, side), jnp.float32),
            pltpu.VMEM((slice_count - 1, windows, modes, 2, side, side), jnp.float32),
            pltpu.SemaphoreType.DMA((slice_count, count)),
            pltpu.SemaphoreType.DMA((slice_count, count)),
        ],
        compiler_params=pltpu.CompilerParams(vmem_limit_bytes=48 << 20),
        name="windows",
    )(row_offset, col_offset, *pieces, probe_modes, amplitude, tables)


def push(src, dst, send_sem, recv_sem, partner):
    return pltpu.make_async_remote_copy(
        src_ref=src,
        dst_ref=dst,
        send_sem=send_sem,
        recv_sem=recv_sem,
        device_id={"tile": partner},
        device_id_type=pl.DeviceIdType.MESH,
    )


def greet(partners):
    barrier = pltpu.get_barrier_semaphore()
    for partner in partners:
        pl.semaphore_signal(
            barrier, inc=1, device_id={"tile": partner}, device_id_type=pl.DeviceIdType.MESH
        )
    pl.semaphore_wait(barrier, len(partners))


def flipped(index, step):
    bit = (index // step) % 2
    return index + step * (1 - 2 * bit), bit


def gather_kernel(tiles, own, first, second, third, fourth, z_out, z_in, y_out, y_in, a_out, a_in, b_out, b_in):
    index = lax.axis_index("tile")
    other_core, core = flipped(index, 2**0)
    other_chip, odd = flipped(index, 2)
    ahead, behind = (index + tiles - 4) % tiles, (index + 4) % tiles
    planes = own.shape[0]
    greet([other_core, other_chip, ahead, behind])

    def far(k):
        return push(own.at[k], fourth.at[k], z_out.at[k], z_in.at[k], ahead)

    def across(source, k):
        return push(source.at[k], second.at[k], y_out.at[k], y_in.at[k], other_chip)

    def beside(source, k):
        return push(source.at[k], first.at[k], a_out.at[k], a_in.at[k], other_core)

    def beside_third(source, k):
        return push(source.at[k], third.at[k], b_out.at[k], b_in.at[k], other_core)

    for k in range(planes):
        far(k).start()

    @pl.when(odd == 1)
    def _():
        for k in range(planes):
            across(own, k).start()

    @pl.when(core == 1)
    def _():
        for k in range(planes):
            beside(own, k).start()

    for k in range(planes + 1):
        if k < planes:
            far(k).wait_recv()

            @pl.when(odd == 0)
            def _():
                across(fourth, k).start()

            @pl.when(core == 0)
            def _():
                beside_third(fourth, k).start()

        if k > 0:
            across(fourth, k - 1).wait_recv()

            @pl.when(core == 0)
            def _():
                beside(second, k - 1).start()

            @pl.when(core == 1)
            def _():
                beside_third(second, k - 1).start()

    for k in range(planes):
        beside(second, k).wait_recv()
        beside_third(second, k).wait_recv()
    for k in range(planes):
        far(k).wait_send()
        across(own, k).wait_send()
        beside(own, k).wait_send()
        beside_third(second, k).wait_send()


def gather_pieces(slices):
    slice_count, parts, rows_here, cols_here = slices.shape
    planes = slice_count * parts
    flat = slices.reshape(planes, rows_here, cols_here)
    anywhere = pl.BlockSpec(memory_space=pl.ANY)
    got = pl.pallas_call(
        functools.partial(gather_kernel, lax.axis_size("tile")),
        out_shape=[jax.ShapeDtypeStruct(flat.shape, jnp.float32)] * 4,
        in_specs=[anywhere],
        out_specs=[anywhere] * 4,
        scratch_shapes=[pltpu.SemaphoreType.DMA((planes,))] * 8,
        compiler_params=pltpu.CompilerParams(collective_id=0, has_side_effects=True),
        name="gather_tiles",
    )(flat)
    return [slices] + [piece.reshape(slices.shape) for piece in got]


def scatter_kernel(tiles, steps, share0, share1, share2, share3, share4, terms, out, terms_out, *refs):
    acc0, acc2, acc4, from_a, from_b, from_chip, from_far, gathered, partial = refs[:9]
    inboxes = refs[9 : 9 + steps]
    load_sem, a_out, a_in, b_out, b_in, y_out, y_in, z_out, z_in, p_out, p_in = refs[9 + steps :]
    index = lax.axis_index("tile")
    other_core, core = flipped(index, 2**0)
    other_chip, odd = flipped(index, 2)
    ahead, behind = (index + tiles - 4) % tiles, (index + 4) % tiles
    planes = share0.shape[0]
    partners, bits = [], []
    for b in range(steps):
        partner, bit = flipped(index, 2**b)
        partners.append(partner)
        bits.append(bit)
    greet([ahead, behind] + partners)

    def beside(k):
        return push(share1.at[k], from_a.at[k], a_out.at[k], a_in.at[k], other_core)

    def beside_third(k):
        return push(share3.at[k], from_b.at[k], b_out.at[k], b_in.at[k], other_core)

    def across(k):
        return push(acc2.at[k], from_chip.at[k], y_out.at[k], y_in.at[k], other_chip)

    def far(k):
        return push(acc4.at[k], from_far.at[k], z_out.at[k], z_in.at[k], behind)

    local = ((share0, acc0), (share2, acc2), (share4, acc4))

    def load(i, k):
        return pltpu.make_async_copy(local[i][0].at[k], local[i][1].at[k], load_sem.at[i, k])

    for k in range(planes):
        beside(k).start()
        beside_third(k).start()
        for i in range(3):
            load(i, k).start()

    bases, sizes = [0], [terms.shape[0]]
    for b in range(steps):
        sizes.append(sizes[-1] // 2)
        bases.append(bases[-1] + bits[b] * sizes[-1])

    def region(b):
        return pl.ds(pl.multiple_of(bases[b], SUBLANES), sizes[b])

    def reduce_copy(b):
        start = bases[b] + (1 - bits[b]) * sizes[b + 1]
        away = pl.ds(pl.multiple_of(start, SUBLANES), sizes[b + 1])
        return push(partial.at[away], inboxes[b], p_out.at[b], p_in.at[b], partners[b])

    def spread_copy(b, base_index):
        part = region(base_index) if base_index is not None else None
        return push(
            gathered.at[part], gathered.at[part], p_out.at[steps + b], p_in.at[steps + b], partners[b]
        )

    partial[...] = terms[...]

    def probe_turn(turn):
        if turn > 2 * steps:
            return
        if 0 < turn <= steps:
            b = turn - 1
            reduce_copy(b).wait_recv()
            partial[region(b + 1)] += inboxes[b][...]
            if turn == steps:
                gathered[region(steps)] = partial[region(steps)]
        elif turn > steps:
            spread_copy(2 * steps - turn, 2 * steps - turn + 1).wait_recv()
        if turn < steps:
            reduce_copy(turn).start()
        elif turn < 2 * steps:
            b = 2 * steps - 1 - turn
            spread_copy(b, b + 1).start()

    for k in range(planes + 1):
        probe_turn(k)
        if k < planes:
            for i in range(3):
                load(i, k).wait()
            beside(k).wait_recv()
            beside_third(k).wait_recv()

            @pl.when(core == 0)
            def _():
                acc2[k] += from_a[k]
                acc4[k] += from_b[k]

            @pl.when(core == 1)
            def _():
                acc2[k] += from_b[k]
                acc0[k] += from_a[k]

            across(k).start()

            @pl.when(odd == 1)
            def _():
                far(k).start()

        if k > 0:
            across(k - 1).wait_recv()

            @pl.when(odd == 0)
            def _():
                acc4[k - 1] += from_chip[k - 1]
                far(k - 1).start()

            @pl.when(odd == 1)
            def _():
                acc0[k - 1] += from_chip[k - 1]

    for turn in range(planes + 1, 2 * steps + 1):
        probe_turn(turn)
    for k in range(planes):
        far(k).wait_recv()
        out[k] = acc0[k] + from_far[k]
    terms_out[...] = gathered[...]
    for k in range(planes):
        beside(k).wait_send()
        beside_third(k).wait_send()
        across(k).wait_send()
        far(k).wait_send()
    for b in range(steps):
        reduce_copy(b).wait_send()
        spread_copy(b, b + 1).wait_send()


def scatter_shares(shares, probe_terms):
    slice_count, parts, rows_here, cols_here = shares[0].shape
    planes = slice_count * parts
    flat_shape = (planes, rows_here, cols_here)
    flat = [share.reshape(flat_shape) for share in shares]
    side = probe_terms.shape[-1]
    terms = probe_terms.reshape(-1, side)
    tiles = lax.axis_size("tile")
    steps = tiles.bit_length() - 1
    assert tiles == 2**steps and tiles > 8
    anywhere = pl.BlockSpec(memory_space=pl.ANY)
    vmem = pl.BlockSpec(memory_space=pltpu.VMEM)
    dma = pltpu.SemaphoreType.DMA
    out, summed = pl.pallas_call(
        functools.partial(scatter_kernel, tiles, steps),
        out_shape=[
            jax.ShapeDtypeStruct(flat_shape, jnp.float32),
            jax.ShapeDtypeStruct(terms.shape, jnp.float32),
        ],
        in_specs=[anywhere] * len(flat) + [vmem],
        out_specs=[vmem, vmem],
        scratch_shapes=[pltpu.VMEM(flat_shape, jnp.float32)] * 7
        + [pltpu.VMEM(terms.shape, jnp.float32)] * 2
        + [pltpu.VMEM((terms.shape[0] >> (b + 1), side), jnp.float32) for b in range(steps)]
        + [dma((3, planes))]
        + [dma((planes,))] * 8
        + [dma((2 * steps,))] * 2,
        compiler_params=pltpu.CompilerParams(
            collective_id=1, has_side_effects=True, vmem_limit_bytes=32 << 20
        ),
        name="scatter_tiles",
    )(*flat, terms)
    return out.reshape(shares[0].shape), summed.reshape(probe_terms.shape)


def on_device(slices, probe_modes, row_offset, col_offset, amplitude):
    side = probe_modes.shape[-1]
    rows_here = slices.shape[2]
    reach = (side - 2) // rows_here + 1
    assert reach == 4
    pieces = gather_pieces(slices)
    *shares, probe_terms = run_windows(pieces, probe_modes, row_offset, col_offset, amplitude)
    return scatter_shares(shares, probe_terms)


def solution(mesh):
    placed = (
        P(None, None, ("scan", "tile"), None),
        P("scan", None, None, None),
        P(("scan", "tile")),
        P(("scan", "tile")),
        P(("scan", "tile"), None, None),
    )
    return jax.shard_map(
        on_device,
        mesh=mesh,
        in_specs=placed,
        out_specs=(P(None, None, ("scan", "tile"), None), P("scan", None, None, None)),
        check_vma=False,
    )
```

```python
import functools

import jax
import jax.numpy as jnp
import numpy as np
from jax import lax
from jax.experimental import pallas as pl
from jax.experimental.pallas import tpu as pltpu
from jax.sharding import PartitionSpec as P

INTENSITY_SHIFT = 0.5
FRESNEL = 0.75
LANES = 128
SUBLANES = 8


def field_tables(side):
    idx = np.arange(side)
    fourier = np.exp(-2j * np.pi * (np.outer(idx, idx) % side) / side) / np.sqrt(side)
    freq = (idx + side // 2) % side - side // 2
    line = np.exp(-1j * np.pi * FRESNEL * freq**2 / (side / 2.0) ** 2)
    propagator = fourier.conj() @ (line[:, None] * fourier)
    blocks = []
    for matrix in (propagator, fourier, fourier.conj(), propagator.conj()):
        block = np.block([[matrix.real, matrix.imag], [-matrix.imag, matrix.real]])
        high = block.astype(np.float32).astype(jnp.bfloat16)
        low = (block - high.astype(np.float64)).astype(np.float32).astype(jnp.bfloat16)
        blocks.append(np.stack([high, low]))
    return np.stack(blocks)


PROP, FWD, INV, PROP_ADJ = range(4)
CONJ = {PROP: PROP_ADJ, FWD: INV, INV: FWD, PROP_ADJ: PROP}


def split_pair(value):
    high = value.astype(jnp.bfloat16)
    low = (value - high.astype(jnp.float32)).astype(jnp.bfloat16)
    return high, low


def two_sided(table_ref, which, fields, side):
    right_high, right_low = table_ref[which, 0], table_ref[which, 1]
    right_mat = jnp.concatenate([right_high, right_low, right_high], axis=0)
    halves = []
    for modes in fields:
        rows = jnp.concatenate([jnp.concatenate([re, im], axis=1) for re, im in modes], axis=0)
        high, low = split_pair(rows)
        lhs = jnp.concatenate([high, high, low], axis=1)
        halves.append(jnp.dot(lhs, right_mat, preferred_element_type=jnp.float32))
    left_high, left_low = table_ref[CONJ[which], 0], table_ref[CONJ[which], 1]
    left_mat = jnp.concatenate([left_high, left_high, left_low], axis=1)
    results = []
    for half, modes in zip(halves, fields):
        count = len(modes)
        high, low = split_pair(half)

        def stack(part):
            pieces = [part[m * side : (m + 1) * side] for m in range(count)]
            return jnp.concatenate(
                [
                    jnp.concatenate([p[:, :side] for p in pieces], axis=1),
                    jnp.concatenate([p[:, side:] for p in pieces], axis=1),
                ],
                axis=0,
            )

        high, low = stack(high), stack(low)
        rhs = jnp.concatenate([high, low, high], axis=0)
        full = jnp.dot(left_mat, rhs, preferred_element_type=jnp.float32)
        results.append(
            [
                (full[:side, m * side : (m + 1) * side], full[side:, m * side : (m + 1) * side])
                for m in range(count)
            ]
        )
    return results


def window_kernel(pieces_count, row_ref, col_ref, *refs):
    pieces = refs[:pieces_count]
    probe_ref, amp_ref, table_ref = refs[pieces_count : pieces_count + 3]
    outs = refs[pieces_count + 3 : 2 * pieces_count + 3]
    probe_out = refs[2 * pieces_count + 3]
    ext, grad, crops, waves, in_sem, out_sem = refs[2 * pieces_count + 4 :]
    slice_count, _, rows_here, cols_here = pieces[0].shape
    windows, side = amp_ref.shape[0], amp_ref.shape[1]
    modes = probe_ref.shape[0]
    col_blocks = cols_here // LANES

    def incoming(s, o):
        return pltpu.make_async_copy(
            pieces[o].at[s], ext.at[s, :, pl.ds(o * rows_here, rows_here)], in_sem.at[s, o]
        )

    def outgoing(s, o):
        return pltpu.make_async_copy(
            grad.at[s, :, pl.ds(o * rows_here, rows_here)], outs[o].at[s], out_sem.at[s, o]
        )

    for s in range(slice_count):
        for o in range(pieces_count):
            incoming(s, o).start()
    grad[...] = jnp.zeros_like(grad)

    tall = side + SUBLANES
    lane = lax.broadcasted_iota(jnp.int32, (tall, LANES), 1)
    margin = jnp.zeros((SUBLANES, LANES), jnp.float32)
    places = []
    for w in range(windows):
        row, col = row_ref[w], col_ref[w]
        block = col // LANES
        shift = col - block * LANES
        first = pl.multiple_of(block * LANES, LANES)
        second = pl.multiple_of(lax.rem(block + 1, col_blocks) * LANES, LANES)
        base = row // SUBLANES * SUBLANES
        places.append((pl.multiple_of(base, SUBLANES), row - base, first, second, shift))

    fields = [[(probe_ref[m, 0], probe_ref[m, 1]) for m in range(modes)] for _ in range(windows)]
    for s in range(slice_count):
        for o in range(pieces_count):
            incoming(s, o).wait()
        exits = []
        for w in range(windows):
            row, lift, first, second, shift = places[w]
            back = lax.rem(LANES - shift, LANES)
            planes = []
            for c in range(2):
                one = pltpu.roll(ext[s, c, pl.ds(row, tall), pl.ds(first, LANES)], back, 1)
                two = pltpu.roll(ext[s, c, pl.ds(row, tall), pl.ds(second, LANES)], back, 1)
                plane = jnp.where(lane < LANES - shift, one, two)
                plane = pltpu.roll(plane, lax.rem(tall - lift, tall), 0)[:side]
                crops[s, w, c] = plane
                planes.append(plane)
            obj_re, obj_im = planes
            chi = []
            for m in range(modes):
                re, im = fields[w][m]
                chi.append((obj_re * re - obj_im * im, obj_re * im + obj_im * re))
            exits.append(chi)
        fields = two_sided(table_ref, PROP if s + 1 < slice_count else FWD, exits, side)
        if s + 1 < slice_count:
            for w in range(windows):
                for m in range(modes):
                    waves[s, w, m, 0] = fields[w][m][0]
                    waves[s, w, m, 1] = fields[w][m][1]

    far_grads = []
    for w in range(windows):
        intensity = sum(re * re + im * im for re, im in fields[w])
        factor = 1.0 - amp_ref[w] / jnp.sqrt(intensity + INTENSITY_SHIFT)
        far_grads.append([(factor * re, factor * im) for re, im in fields[w]])
    fields = two_sided(table_ref, INV, far_grads, side)

    for s in reversed(range(slice_count)):
        wave_grads = []
        for w in range(windows):
            row, lift, first, second, shift = places[w]
            obj_re, obj_im = crops[s, w, 0], crops[s, w, 1]
            grad_re = jnp.zeros((side, side), jnp.float32)
            grad_im = jnp.zeros((side, side), jnp.float32)
            terms = []
            for m in range(modes):
                re, im = fields[w][m]
                if s == 0:
                    wave_re, wave_im = probe_ref[m, 0], probe_ref[m, 1]
                else:
                    wave_re, wave_im = waves[s - 1, w, m, 0], waves[s - 1, w, m, 1]
                grad_re += re * wave_re + im * wave_im
                grad_im += im * wave_re - re * wave_im
                terms.append((re * obj_re + im * obj_im, im * obj_re - re * obj_im))
            wave_grads.append(terms)
            for c, plane in enumerate((grad_re, grad_im)):
                turned = pltpu.roll(jnp.concatenate([plane, margin], axis=0), lift, 0)
                turned = pltpu.roll(turned, shift, 1)
                low = jnp.where(lane >= shift, turned, 0.0)
                grad[s, c, pl.ds(row, tall), pl.ds(first, LANES)] += low
                high = jnp.where(lane < shift, turned, 0.0)
                grad[s, c, pl.ds(row, tall), pl.ds(second, LANES)] += high
        for o in range(pieces_count):
            outgoing(s, o).start()
        if s > 0:
            fields = two_sided(table_ref, PROP_ADJ, wave_grads, side)
    for m in range(modes):
        for c in range(2):
            probe_out[m, c] = sum(wave_grads[w][m][c] for w in range(windows))
    for s in range(slice_count):
        for o in range(pieces_count):
            outgoing(s, o).wait()


def run_windows(pieces, probe_modes, row_offset, col_offset, amplitude):
    count = len(pieces)
    slice_count, parts, rows_here, cols_here = pieces[0].shape
    windows, side = amplitude.shape[0], amplitude.shape[1]
    modes = probe_modes.shape[0]
    tables = jnp.asarray(field_tables(side))
    anywhere = pl.BlockSpec(memory_space=pl.ANY)
    vmem = pl.BlockSpec(memory_space=pltpu.VMEM)
    smem = pl.BlockSpec(memory_space=pltpu.SMEM)
    total = count * rows_here
    return pl.pallas_call(
        functools.partial(window_kernel, count),
        out_shape=[jax.ShapeDtypeStruct(p.shape, jnp.float32) for p in pieces]
        + [jax.ShapeDtypeStruct(probe_modes.shape, jnp.float32)],
        in_specs=[smem, smem] + [anywhere] * count + [vmem] * 3,
        out_specs=[anywhere] * count + [vmem],
        scratch_shapes=[
            pltpu.VMEM((slice_count, parts, total, cols_here), jnp.float32),
            pltpu.VMEM((slice_count, parts, total, cols_here), jnp.float32),
            pltpu.VMEM((slice_count, windows, parts, side, side), jnp.float32),
            pltpu.VMEM((slice_count - 1, windows, modes, 2, side, side), jnp.float32),
            pltpu.SemaphoreType.DMA((slice_count, count)),
            pltpu.SemaphoreType.DMA((slice_count, count)),
        ],
        compiler_params=pltpu.CompilerParams(vmem_limit_bytes=48 << 20),
        name="windows",
    )(row_offset, col_offset, *pieces, probe_modes, amplitude, tables)


def push(src, dst, send_sem, recv_sem, partner):
    return pltpu.make_async_remote_copy(
        src_ref=src,
        dst_ref=dst,
        send_sem=send_sem,
        recv_sem=recv_sem,
        device_id={"tile": partner},
        device_id_type=pl.DeviceIdType.MESH,
    )


def greet(partners):
    barrier = pltpu.get_barrier_semaphore()
    for partner in partners:
        pl.semaphore_signal(
            barrier, inc=1, device_id={"tile": partner}, device_id_type=pl.DeviceIdType.MESH
        )
    pl.semaphore_wait(barrier, len(partners))


def flipped(index, step):
    bit = (index // step) % 2
    return index + step * (1 - 2 * bit), bit


def gather_kernel(tiles, own, first, second, third, fourth, z_out, z_in, y_out, y_in, a_out, a_in, b_out, b_in):
    index = lax.axis_index("tile")
    other_core, core = flipped(index, 2**0)
    other_chip, odd = flipped(index, 2)
    ahead, behind = (index + tiles - 4) % tiles, (index + 4) % tiles
    planes = own.shape[0]
    greet([other_core, other_chip, ahead, behind])

    def far(k):
        return push(own.at[k], fourth.at[k], z_out.at[k], z_in.at[k], ahead)

    def across(source, k):
        return push(source.at[k], second.at[k], y_out.at[k], y_in.at[k], other_chip)

    def beside(source, k):
        return push(source.at[k], first.at[k], a_out.at[k], a_in.at[k], other_core)

    def beside_third(source, k):
        return push(source.at[k], third.at[k], b_out.at[k], b_in.at[k], other_core)

    for k in range(planes):
        far(k).start()

    @pl.when(odd == 1)
    def _():
        for k in range(planes):
            across(own, k).start()

    @pl.when(core == 1)
    def _():
        for k in range(planes):
            beside(own, k).start()

    for k in range(planes + 1):
        if k < planes:
            far(k).wait_recv()

            @pl.when(odd == 0)
            def _():
                across(fourth, k).start()

            @pl.when(core == 0)
            def _():
                beside_third(fourth, k).start()

        if k > 0:
            across(fourth, k - 1).wait_recv()

            @pl.when(core == 0)
            def _():
                beside(second, k - 1).start()

            @pl.when(core == 1)
            def _():
                beside_third(second, k - 1).start()

    for k in range(planes):
        beside(second, k).wait_recv()
        beside_third(second, k).wait_recv()
    for k in range(planes):
        far(k).wait_send()
        across(own, k).wait_send()
        beside(own, k).wait_send()
        beside_third(second, k).wait_send()


def gather_pieces(slices):
    slice_count, parts, rows_here, cols_here = slices.shape
    planes = slice_count * parts
    flat = slices.reshape(planes, rows_here, cols_here)
    anywhere = pl.BlockSpec(memory_space=pl.ANY)
    got = pl.pallas_call(
        functools.partial(gather_kernel, lax.axis_size("tile")),
        out_shape=[jax.ShapeDtypeStruct(flat.shape, jnp.float32)] * 4,
        in_specs=[anywhere],
        out_specs=[anywhere] * 4,
        scratch_shapes=[pltpu.SemaphoreType.DMA((planes,))] * 8,
        compiler_params=pltpu.CompilerParams(collective_id=0, has_side_effects=True),
        name="gather_tiles",
    )(flat)
    return [slices] + [piece.reshape(slices.shape) for piece in got]


def scatter_kernel(tiles, steps, share0, share1, share2, share3, share4, terms, out, terms_out, *refs):
    acc0, acc2, acc4, from_a, from_b, from_chip, from_far, gathered, partial = refs[:9]
    inboxes = refs[9 : 9 + steps]
    load_sem, a_out, a_in, b_out, b_in, y_out, y_in, z_out, z_in, p_out, p_in = refs[9 + steps :]
    index = lax.axis_index("tile")
    other_core, core = flipped(index, 2**0)
    other_chip, odd = flipped(index, 2)
    ahead, behind = (index + tiles - 4) % tiles, (index + 4) % tiles
    planes = share0.shape[0]
    partners, bits = [], []
    for b in range(steps):
        partner, bit = flipped(index, 2**b)
        partners.append(partner)
        bits.append(bit)
    greet([ahead, behind] + partners)

    def beside(k):
        return push(share1.at[k], from_a.at[k], a_out.at[k], a_in.at[k], other_core)

    def beside_third(k):
        return push(share3.at[k], from_b.at[k], b_out.at[k], b_in.at[k], other_core)

    def across(k):
        return push(acc2.at[k], from_chip.at[k], y_out.at[k], y_in.at[k], other_chip)

    def far(k):
        return push(acc4.at[k], from_far.at[k], z_out.at[k], z_in.at[k], behind)

    local = ((share0, acc0), (share2, acc2), (share4, acc4))

    def load(i, k):
        return pltpu.make_async_copy(local[i][0].at[k], local[i][1].at[k], load_sem.at[i, k])

    bases, sizes = [0], [terms.shape[0]]
    for b in range(steps):
        sizes.append(sizes[-1] // 2)
        bases.append(bases[-1] + bits[b] * sizes[-1])

    def region(b):
        return pl.ds(pl.multiple_of(bases[b], SUBLANES), sizes[b])

    def reduce_copy(b):
        start = bases[b] + (1 - bits[b]) * sizes[b + 1]
        away = pl.ds(pl.multiple_of(start, SUBLANES), sizes[b + 1])
        return push(partial.at[away], inboxes[b], p_out.at[b], p_in.at[b], partners[b])

    def spread_copy(b, base_index):
        part = region(base_index) if base_index is not None else None
        return push(
            gathered.at[part], gathered.at[part], p_out.at[steps + b], p_in.at[steps + b], partners[b]
        )

    partial[...] = terms[...]

    def probe_turn(turn):
        if turn > 2 * steps:
            return
        if 0 < turn <= steps:
            b = turn - 1
            reduce_copy(b).wait_recv()
            partial[region(b + 1)] += inboxes[b][...]
            if turn == steps:
                gathered[region(steps)] = partial[region(steps)]
        elif turn > steps:
            spread_copy(2 * steps - turn, 2 * steps - turn + 1).wait_recv()
        if turn < steps:
            reduce_copy(turn).start()
        elif turn < 2 * steps:
            b = 2 * steps - 1 - turn
            spread_copy(b, b + 1).start()

    probe_turn(0)
    for k in range(planes):
        beside(k).start()
        beside_third(k).start()
        for i in range(3):
            load(i, k).start()

    probe_turn(1)
    for k in range(planes):
        for i in range(3):
            load(i, k).wait()
        beside(k).wait_recv()
        beside_third(k).wait_recv()

        @pl.when(core == 0)
        def _():
            acc2[k] += from_a[k]
            acc4[k] += from_b[k]

        @pl.when(core == 1)
        def _():
            acc2[k] += from_b[k]
            acc0[k] += from_a[k]

        across(k).start()

    turn_before = {0: 2, 1: 3, 3: 4, 4: 5, 5: 6}
    for k in range(planes):
        if k in turn_before:
            probe_turn(turn_before[k])
        if k == 0:

            @pl.when(odd == 1)
            def _():
                far(0).start()

        across(k).wait_recv()

        @pl.when(odd == 0)
        def _():
            acc4[k] += from_chip[k]
            far(k).start()

        @pl.when(odd == 1)
        def _():
            acc0[k] += from_chip[k]
            if k + 1 < planes:
                far(k + 1).start()

    for turn in range(7, 2 * steps):
        probe_turn(turn)
    for k in range(planes):
        if k == planes - 1:
            probe_turn(2 * steps)
        far(k).wait_recv()
        out[k] = acc0[k] + from_far[k]
    terms_out[...] = gathered[...]
    for k in range(planes):
        beside(k).wait_send()
        beside_third(k).wait_send()
        across(k).wait_send()
        far(k).wait_send()
    for b in range(steps):
        reduce_copy(b).wait_send()
        spread_copy(b, b + 1).wait_send()


def scatter_shares(shares, probe_terms):
    slice_count, parts, rows_here, cols_here = shares[0].shape
    planes = slice_count * parts
    flat_shape = (planes, rows_here, cols_here)
    flat = [share.reshape(flat_shape) for share in shares]
    side = probe_terms.shape[-1]
    terms = probe_terms.reshape(-1, side)
    tiles = lax.axis_size("tile")
    steps = tiles.bit_length() - 1
    assert tiles == 2**steps and tiles > 8
    anywhere = pl.BlockSpec(memory_space=pl.ANY)
    vmem = pl.BlockSpec(memory_space=pltpu.VMEM)
    dma = pltpu.SemaphoreType.DMA
    out, summed = pl.pallas_call(
        functools.partial(scatter_kernel, tiles, steps),
        out_shape=[
            jax.ShapeDtypeStruct(flat_shape, jnp.float32),
            jax.ShapeDtypeStruct(terms.shape, jnp.float32),
        ],
        in_specs=[anywhere] * len(flat) + [vmem],
        out_specs=[vmem, vmem],
        scratch_shapes=[pltpu.VMEM(flat_shape, jnp.float32)] * 7
        + [pltpu.VMEM(terms.shape, jnp.float32)] * 2
        + [pltpu.VMEM((terms.shape[0] >> (b + 1), side), jnp.float32) for b in range(steps)]
        + [dma((3, planes))]
        + [dma((planes,))] * 8
        + [dma((2 * steps,))] * 2,
        compiler_params=pltpu.CompilerParams(
            collective_id=1, has_side_effects=True, vmem_limit_bytes=32 << 20
        ),
        name="scatter_tiles",
    )(*flat, terms)
    return out.reshape(shares[0].shape), summed.reshape(probe_terms.shape)


def on_device(slices, probe_modes, row_offset, col_offset, amplitude):
    side = probe_modes.shape[-1]
    rows_here = slices.shape[2]
    reach = (side - 2) // rows_here + 1
    assert reach == 4
    pieces = gather_pieces(slices)
    *shares, probe_terms = run_windows(pieces, probe_modes, row_offset, col_offset, amplitude)
    return scatter_shares(shares, probe_terms)


def solution(mesh):
    placed = (
        P(None, None, ("scan", "tile"), None),
        P("scan", None, None, None),
        P(("scan", "tile")),
        P(("scan", "tile")),
        P(("scan", "tile"), None, None),
    )
    return jax.shard_map(
        on_device,
        mesh=mesh,
        in_specs=placed,
        out_specs=(P(None, None, ("scan", "tile"), None), P("scan", None, None, None)),
        check_vma=False,
    )
```

```python
import functools

import jax
import jax.numpy as jnp
import numpy as np
from jax import lax
from jax.experimental import pallas as pl
from jax.experimental.pallas import tpu as pltpu
from jax.sharding import PartitionSpec as P

INTENSITY_SHIFT = 0.5
FRESNEL = 0.75
LANES = 128
SUBLANES = 8
CUTS = 2


def field_tables(side):
    idx = np.arange(side)
    fourier = np.exp(-2j * np.pi * (np.outer(idx, idx) % side) / side) / np.sqrt(side)
    freq = (idx + side // 2) % side - side // 2
    line = np.exp(-1j * np.pi * FRESNEL * freq**2 / (side / 2.0) ** 2)
    propagator = fourier.conj() @ (line[:, None] * fourier)
    blocks = []
    for matrix in (propagator, fourier, fourier.conj(), propagator.conj()):
        block = np.block([[matrix.real, matrix.imag], [-matrix.imag, matrix.real]])
        high = block.astype(np.float32).astype(jnp.bfloat16)
        low = (block - high.astype(np.float64)).astype(np.float32).astype(jnp.bfloat16)
        blocks.append(np.stack([high, low]))
    return np.stack(blocks)


PROP, FWD, INV, PROP_ADJ = range(4)
CONJ = {PROP: PROP_ADJ, FWD: INV, INV: FWD, PROP_ADJ: PROP}


def split_pair(value):
    high = value.astype(jnp.bfloat16)
    low = (value - high.astype(jnp.float32)).astype(jnp.bfloat16)
    return high, low


def two_sided(table_ref, which, fields, side):
    right_high, right_low = table_ref[which, 0], table_ref[which, 1]
    right_mat = jnp.concatenate([right_high, right_low, right_high], axis=0)
    halves = []
    for modes in fields:
        rows = jnp.concatenate([jnp.concatenate([re, im], axis=1) for re, im in modes], axis=0)
        high, low = split_pair(rows)
        lhs = jnp.concatenate([high, high, low], axis=1)
        halves.append(jnp.dot(lhs, right_mat, preferred_element_type=jnp.float32))
    left_high, left_low = table_ref[CONJ[which], 0], table_ref[CONJ[which], 1]
    left_mat = jnp.concatenate([left_high, left_high, left_low], axis=1)
    results = []
    for half, modes in zip(halves, fields):
        count = len(modes)
        high, low = split_pair(half)

        def stack(part):
            pieces = [part[m * side : (m + 1) * side] for m in range(count)]
            return jnp.concatenate(
                [
                    jnp.concatenate([p[:, :side] for p in pieces], axis=1),
                    jnp.concatenate([p[:, side:] for p in pieces], axis=1),
                ],
                axis=0,
            )

        high, low = stack(high), stack(low)
        rhs = jnp.concatenate([high, low, high], axis=0)
        full = jnp.dot(left_mat, rhs, preferred_element_type=jnp.float32)
        results.append(
            [
                (full[:side, m * side : (m + 1) * side], full[side:, m * side : (m + 1) * side])
                for m in range(count)
            ]
        )
    return results


def window_kernel(pieces_count, row_ref, col_ref, *refs):
    pieces = refs[:pieces_count]
    probe_ref, amp_ref, table_ref = refs[pieces_count : pieces_count + 3]
    outs = refs[pieces_count + 3 : 2 * pieces_count + 3]
    probe_out = refs[2 * pieces_count + 3]
    ext, grad, crops, waves, in_sem, out_sem = refs[2 * pieces_count + 4 :]
    slice_count, _, rows_here, cols_here = pieces[0].shape
    windows, side = amp_ref.shape[0], amp_ref.shape[1]
    modes = probe_ref.shape[0]
    col_blocks = cols_here // LANES

    def incoming(s, o):
        return pltpu.make_async_copy(
            pieces[o].at[s], ext.at[s, :, pl.ds(o * rows_here, rows_here)], in_sem.at[s, o]
        )

    def outgoing(s, o):
        return pltpu.make_async_copy(
            grad.at[s, :, pl.ds(o * rows_here, rows_here)], outs[o].at[s], out_sem.at[s, o]
        )

    for s in range(slice_count):
        for o in range(pieces_count):
            incoming(s, o).start()
    grad[...] = jnp.zeros_like(grad)

    tall = side + SUBLANES
    lane = lax.broadcasted_iota(jnp.int32, (tall, LANES), 1)
    margin = jnp.zeros((SUBLANES, LANES), jnp.float32)
    places = []
    for w in range(windows):
        row, col = row_ref[w], col_ref[w]
        block = col // LANES
        shift = col - block * LANES
        first = pl.multiple_of(block * LANES, LANES)
        second = pl.multiple_of(lax.rem(block + 1, col_blocks) * LANES, LANES)
        base = row // SUBLANES * SUBLANES
        places.append((pl.multiple_of(base, SUBLANES), row - base, first, second, shift))

    fields = [[(probe_ref[m, 0], probe_ref[m, 1]) for m in range(modes)] for _ in range(windows)]
    for s in range(slice_count):
        for o in range(pieces_count):
            incoming(s, o).wait()
        exits = []
        for w in range(windows):
            row, lift, first, second, shift = places[w]
            back = lax.rem(LANES - shift, LANES)
            planes = []
            for c in range(2):
                one = pltpu.roll(ext[s, c, pl.ds(row, tall), pl.ds(first, LANES)], back, 1)
                two = pltpu.roll(ext[s, c, pl.ds(row, tall), pl.ds(second, LANES)], back, 1)
                plane = jnp.where(lane < LANES - shift, one, two)
                plane = pltpu.roll(plane, lax.rem(tall - lift, tall), 0)[:side]
                crops[s, w, c] = plane
                planes.append(plane)
            obj_re, obj_im = planes
            chi = []
            for m in range(modes):
                re, im = fields[w][m]
                chi.append((obj_re * re - obj_im * im, obj_re * im + obj_im * re))
            exits.append(chi)
        fields = two_sided(table_ref, PROP if s + 1 < slice_count else FWD, exits, side)
        if s + 1 < slice_count:
            for w in range(windows):
                for m in range(modes):
                    waves[s, w, m, 0] = fields[w][m][0]
                    waves[s, w, m, 1] = fields[w][m][1]

    far_grads = []
    for w in range(windows):
        intensity = sum(re * re + im * im for re, im in fields[w])
        factor = 1.0 - amp_ref[w] / jnp.sqrt(intensity + INTENSITY_SHIFT)
        far_grads.append([(factor * re, factor * im) for re, im in fields[w]])
    fields = two_sided(table_ref, INV, far_grads, side)

    for s in reversed(range(slice_count)):
        wave_grads = []
        for w in range(windows):
            row, lift, first, second, shift = places[w]
            obj_re, obj_im = crops[s, w, 0], crops[s, w, 1]
            grad_re = jnp.zeros((side, side), jnp.float32)
            grad_im = jnp.zeros((side, side), jnp.float32)
            terms = []
            for m in range(modes):
                re, im = fields[w][m]
                if s == 0:
                    wave_re, wave_im = probe_ref[m, 0], probe_ref[m, 1]
                else:
                    wave_re, wave_im = waves[s - 1, w, m, 0], waves[s - 1, w, m, 1]
                grad_re += re * wave_re + im * wave_im
                grad_im += im * wave_re - re * wave_im
                terms.append((re * obj_re + im * obj_im, im * obj_re - re * obj_im))
            wave_grads.append(terms)
            for c, plane in enumerate((grad_re, grad_im)):
                turned = pltpu.roll(jnp.concatenate([plane, margin], axis=0), lift, 0)
                turned = pltpu.roll(turned, shift, 1)
                low = jnp.where(lane >= shift, turned, 0.0)
                grad[s, c, pl.ds(row, tall), pl.ds(first, LANES)] += low
                high = jnp.where(lane < shift, turned, 0.0)
                grad[s, c, pl.ds(row, tall), pl.ds(second, LANES)] += high
        for o in range(pieces_count):
            outgoing(s, o).start()
        if s > 0:
            fields = two_sided(table_ref, PROP_ADJ, wave_grads, side)
    for m in range(modes):
        for c in range(2):
            probe_out[m, c] = sum(wave_grads[w][m][c] for w in range(windows))
    for s in range(slice_count):
        for o in range(pieces_count):
            outgoing(s, o).wait()


def run_windows(pieces, probe_modes, row_offset, col_offset, amplitude):
    count = len(pieces)
    slice_count, parts, rows_here, cols_here = pieces[0].shape
    windows, side = amplitude.shape[0], amplitude.shape[1]
    modes = probe_modes.shape[0]
    tables = jnp.asarray(field_tables(side))
    anywhere = pl.BlockSpec(memory_space=pl.ANY)
    vmem = pl.BlockSpec(memory_space=pltpu.VMEM)
    smem = pl.BlockSpec(memory_space=pltpu.SMEM)
    total = count * rows_here
    return pl.pallas_call(
        functools.partial(window_kernel, count),
        out_shape=[jax.ShapeDtypeStruct(p.shape, jnp.float32) for p in pieces]
        + [jax.ShapeDtypeStruct(probe_modes.shape, jnp.float32)],
        in_specs=[smem, smem] + [anywhere] * count + [vmem] * 3,
        out_specs=[anywhere] * count + [vmem],
        scratch_shapes=[
            pltpu.VMEM((slice_count, parts, total, cols_here), jnp.float32),
            pltpu.VMEM((slice_count, parts, total, cols_here), jnp.float32),
            pltpu.VMEM((slice_count, windows, parts, side, side), jnp.float32),
            pltpu.VMEM((slice_count - 1, windows, modes, 2, side, side), jnp.float32),
            pltpu.SemaphoreType.DMA((slice_count, count)),
            pltpu.SemaphoreType.DMA((slice_count, count)),
        ],
        compiler_params=pltpu.CompilerParams(vmem_limit_bytes=48 << 20),
        name="windows",
    )(row_offset, col_offset, *pieces, probe_modes, amplitude, tables)


def push(src, dst, send_sem, recv_sem, partner):
    return pltpu.make_async_remote_copy(
        src_ref=src,
        dst_ref=dst,
        send_sem=send_sem,
        recv_sem=recv_sem,
        device_id={"tile": partner},
        device_id_type=pl.DeviceIdType.MESH,
    )


def greet(partners):
    barrier = pltpu.get_barrier_semaphore()
    for partner in partners:
        pl.semaphore_signal(
            barrier, inc=1, device_id={"tile": partner}, device_id_type=pl.DeviceIdType.MESH
        )
    pl.semaphore_wait(barrier, len(partners))


def flipped(index, step):
    bit = (index // step) % 2
    return index + step * (1 - 2 * bit), bit


def gather_kernel(tiles, own, first, second, third, fourth, z_out, z_in, y_out, y_in, a_out, a_in, b_out, b_in):
    index = lax.axis_index("tile")
    other_core, core = flipped(index, 2**0)
    other_chip, odd = flipped(index, 2)
    ahead, behind = (index + tiles - 4) % tiles, (index + 4) % tiles
    planes = own.shape[0]
    greet([other_core, other_chip, ahead, behind])

    def far(k):
        return push(own.at[k], fourth.at[k], z_out.at[k], z_in.at[k], ahead)

    def across(source, k):
        return push(source.at[k], second.at[k], y_out.at[k], y_in.at[k], other_chip)

    def beside(source, k):
        return push(source.at[k], first.at[k], a_out.at[k], a_in.at[k], other_core)

    def beside_third(source, k):
        return push(source.at[k], third.at[k], b_out.at[k], b_in.at[k], other_core)

    for k in range(planes):
        far(k).start()

    @pl.when(odd == 1)
    def _():
        for k in range(planes):
            across(own, k).start()

    @pl.when(core == 1)
    def _():
        for k in range(planes):
            beside(own, k).start()

    for k in range(planes + 1):
        if k < planes:
            far(k).wait_recv()

            @pl.when(odd == 0)
            def _():
                across(fourth, k).start()

            @pl.when(core == 0)
            def _():
                beside_third(fourth, k).start()

        if k > 0:
            across(fourth, k - 1).wait_recv()

            @pl.when(core == 0)
            def _():
                beside(second, k - 1).start()

            @pl.when(core == 1)
            def _():
                beside_third(second, k - 1).start()

    for k in range(planes):
        beside(second, k).wait_recv()
        beside_third(second, k).wait_recv()
    for k in range(planes):
        far(k).wait_send()
        across(own, k).wait_send()
        beside(own, k).wait_send()
        beside_third(second, k).wait_send()


def gather_pieces(slices):
    slice_count, parts, rows_here, cols_here = slices.shape
    planes = slice_count * parts * CUTS
    flat = slices.reshape(planes, rows_here // CUTS, cols_here)
    anywhere = pl.BlockSpec(memory_space=pl.ANY)
    got = pl.pallas_call(
        functools.partial(gather_kernel, lax.axis_size("tile")),
        out_shape=[jax.ShapeDtypeStruct(flat.shape, jnp.float32)] * 4,
        in_specs=[anywhere],
        out_specs=[anywhere] * 4,
        scratch_shapes=[pltpu.SemaphoreType.DMA((planes,))] * 8,
        compiler_params=pltpu.CompilerParams(collective_id=0, has_side_effects=True),
        name="gather_tiles",
    )(flat)
    return [slices] + [piece.reshape(slices.shape) for piece in got]


def scatter_kernel(tiles, steps, share0, share1, share2, share3, share4, terms, out, terms_out, *refs):
    acc0, acc2, acc4, from_a, from_b, from_chip, from_far, gathered, partial = refs[:9]
    inboxes = refs[9 : 9 + steps]
    load_sem, a_out, a_in, b_out, b_in, y_out, y_in, z_out, z_in, p_out, p_in = refs[9 + steps :]
    index = lax.axis_index("tile")
    other_core, core = flipped(index, 2**0)
    other_chip, odd = flipped(index, 2)
    ahead, behind = (index + tiles - 4) % tiles, (index + 4) % tiles
    planes = share0.shape[0]
    partners, bits = [], []
    for b in range(steps):
        partner, bit = flipped(index, 2**b)
        partners.append(partner)
        bits.append(bit)
    greet([ahead, behind] + partners)

    def beside(k):
        return push(share1.at[k], from_a.at[k], a_out.at[k], a_in.at[k], other_core)

    def beside_third(k):
        return push(share3.at[k], from_b.at[k], b_out.at[k], b_in.at[k], other_core)

    def across(k):
        return push(acc2.at[k], from_chip.at[k], y_out.at[k], y_in.at[k], other_chip)

    def far(k):
        return push(acc4.at[k], from_far.at[k], z_out.at[k], z_in.at[k], behind)

    local = ((share0, acc0), (share2, acc2), (share4, acc4))

    def load(i, k):
        return pltpu.make_async_copy(local[i][0].at[k], local[i][1].at[k], load_sem.at[i, k])

    bases, sizes = [0], [terms.shape[0]]
    for b in range(steps):
        sizes.append(sizes[-1] // 2)
        bases.append(bases[-1] + bits[b] * sizes[-1])

    def region(b):
        return pl.ds(pl.multiple_of(bases[b], SUBLANES), sizes[b])

    def reduce_copy(b):
        start = bases[b] + (1 - bits[b]) * sizes[b + 1]
        away = pl.ds(pl.multiple_of(start, SUBLANES), sizes[b + 1])
        return push(partial.at[away], inboxes[b], p_out.at[b], p_in.at[b], partners[b])

    def spread_copy(b, base_index):
        part = region(base_index) if base_index is not None else None
        return push(
            gathered.at[part], gathered.at[part], p_out.at[steps + b], p_in.at[steps + b], partners[b]
        )

    partial[...] = terms[...]

    def probe_turn(turn):
        if turn > 2 * steps:
            return
        if 0 < turn <= steps:
            b = turn - 1
            reduce_copy(b).wait_recv()
            partial[region(b + 1)] += inboxes[b][...]
            if turn == steps:
                gathered[region(steps)] = partial[region(steps)]
        elif turn > steps:
            spread_copy(2 * steps - turn, 2 * steps - turn + 1).wait_recv()
        if turn < steps:
            reduce_copy(turn).start()
        elif turn < 2 * steps:
            b = 2 * steps - 1 - turn
            spread_copy(b, b + 1).start()

    probe_turn(0)
    for k in range(planes):
        beside(k).start()
        beside_third(k).start()
        for i in range(3):
            load(i, k).start()

    probe_turn(1)
    for k in range(planes):
        for i in range(3):
            load(i, k).wait()
        beside(k).wait_recv()
        beside_third(k).wait_recv()

        @pl.when(core == 0)
        def _():
            acc2[k] += from_a[k]
            acc4[k] += from_b[k]

        @pl.when(core == 1)
        def _():
            acc2[k] += from_b[k]
            acc0[k] += from_a[k]

        across(k).start()

    turn_before = {0: 2, 2: 3, 5: 4, 7: 5, 9: 6}
    for k in range(planes):
        if k in turn_before:
            probe_turn(turn_before[k])
        if k == 0:

            @pl.when(odd == 1)
            def _():
                far(0).start()

        across(k).wait_recv()

        @pl.when(odd == 0)
        def _():
            acc4[k] += from_chip[k]
            far(k).start()

        @pl.when(odd == 1)
        def _():
            acc0[k] += from_chip[k]
            if k + 1 < planes:
                far(k + 1).start()

    for turn in range(7, 2 * steps):
        probe_turn(turn)
    for k in range(planes):
        if k == planes - 1:
            probe_turn(2 * steps)
        far(k).wait_recv()
        out[k] = acc0[k] + from_far[k]
    terms_out[...] = gathered[...]
    for k in range(planes):
        beside(k).wait_send()
        beside_third(k).wait_send()
        across(k).wait_send()
        far(k).wait_send()
    for b in range(steps):
        reduce_copy(b).wait_send()
        spread_copy(b, b + 1).wait_send()


def scatter_shares(shares, probe_terms):
    slice_count, parts, rows_here, cols_here = shares[0].shape
    planes = slice_count * parts * CUTS
    flat_shape = (planes, rows_here // CUTS, cols_here)
    flat = [share.reshape(flat_shape) for share in shares]
    side = probe_terms.shape[-1]
    terms = probe_terms.reshape(-1, side)
    tiles = lax.axis_size("tile")
    steps = tiles.bit_length() - 1
    assert tiles == 2**steps and tiles > 8
    anywhere = pl.BlockSpec(memory_space=pl.ANY)
    vmem = pl.BlockSpec(memory_space=pltpu.VMEM)
    dma = pltpu.SemaphoreType.DMA
    out, summed = pl.pallas_call(
        functools.partial(scatter_kernel, tiles, steps),
        out_shape=[
            jax.ShapeDtypeStruct(flat_shape, jnp.float32),
            jax.ShapeDtypeStruct(terms.shape, jnp.float32),
        ],
        in_specs=[anywhere] * len(flat) + [vmem],
        out_specs=[vmem, vmem],
        scratch_shapes=[pltpu.VMEM(flat_shape, jnp.float32)] * 7
        + [pltpu.VMEM(terms.shape, jnp.float32)] * 2
        + [pltpu.VMEM((terms.shape[0] >> (b + 1), side), jnp.float32) for b in range(steps)]
        + [dma((3, planes))]
        + [dma((planes,))] * 8
        + [dma((2 * steps,))] * 2,
        compiler_params=pltpu.CompilerParams(
            collective_id=1, has_side_effects=True, vmem_limit_bytes=32 << 20
        ),
        name="scatter_tiles",
    )(*flat, terms)
    return out.reshape(shares[0].shape), summed.reshape(probe_terms.shape)


def on_device(slices, probe_modes, row_offset, col_offset, amplitude):
    side = probe_modes.shape[-1]
    rows_here = slices.shape[2]
    reach = (side - 2) // rows_here + 1
    assert reach == 4
    pieces = gather_pieces(slices)
    *shares, probe_terms = run_windows(pieces, probe_modes, row_offset, col_offset, amplitude)
    return scatter_shares(shares, probe_terms)


def solution(mesh):
    placed = (
        P(None, None, ("scan", "tile"), None),
        P("scan", None, None, None),
        P(("scan", "tile")),
        P(("scan", "tile")),
        P(("scan", "tile"), None, None),
    )
    return jax.shard_map(
        on_device,
        mesh=mesh,
        in_specs=placed,
        out_specs=(P(None, None, ("scan", "tile"), None), P("scan", None, None, None)),
        check_vma=False,
    )
```
